32 devices in a mesh: bin: 8 (over z, y), sky: 4 (over x, core).
Axes of the slice: x: 2, y: 2, z: 4, core: 2. Of those that a mesh axis runs over, the one named last changes fastest.
Arguments:
- lensing_maps: bfloat16 [8, 32, 8192], P('bin', 'sky')
- filter_taps: float32 [5, 17], replicated, may hold values from -1.5 to 1.5
- survey_mask: int32 [4, 64], P('sky'), may hold values 0 or 1
- bin_pairs: int32 [36, 2], replicated, may hold values from 0 to 7, as said below
- target_corr: float32 [36, 5, 4], replicated, may hold values from -3 to 3
- pair_weight: float32 [36, 5, 4], replicated, may hold values from 0.3 to 3
Outputs:
- corr_table: float32 [36, 5, 4], replicated
- map_gradient: float32 [8, 32, 8192], P('bin', 'sky')
The draws below stay inside these ranges and needn't reach their ends.
Inputs may be any that keep to these rules, and one draw needn't show every extreme that they name: `bin_pairs`: every unordered pair of the 8 bins, a bin with itself included, is listed exactly once; the order of the list and of the two bins in a row vary.
All inputs are finite; a program needn't handle non-finite values. No bound on the sum of `survey_mask` on one device may be relied on, other than what follows from the above.
Results may differ from the reference program's by a relative error of at most 0.0015.
Values may be sent and summed in bfloat16 or wider, within the bound.
A program may use at most 64 MiB of HBM per device.

```python
import math
import jax
import jax.numpy as jnp
import numpy as np
from jax import lax

BINS = 8
PAIRS = 36
SCALES = 5
HALF = 8
LAGS = 4
NY = 8192
NX = 32


def draw_lensing_maps(key, part):
    amplitude = jax.random.uniform(jax.random.fold_in(key, 3), (BINS, 1, 1), jnp.float32, 0.5, 0.95)
    shared = jax.random.normal(jax.random.fold_in(key, 1), (NX, NY), jnp.float32)
    single = jax.random.normal(jax.random.fold_in(key, 2), (BINS, NX, NY), jnp.float32)
    mixed = amplitude * shared[None] + jnp.sqrt(1.0 - amplitude * amplitude) * single
    return mixed.astype(jnp.bfloat16)


def draw_bin_pairs(key, part):
    upper_row, upper_col = np.triu_indices(BINS)
    ordering = jax.random.permutation(jax.random.fold_in(key, 11), PAIRS)
    flipped = jax.random.randint(jax.random.fold_in(key, 12), (PAIRS,), 0, 2)
    left_bin = jnp.asarray(upper_row, jnp.int32)[ordering]
    right_bin = jnp.asarray(upper_col, jnp.int32)[ordering]
    first_bin = jnp.where(flipped == 1, right_bin, left_bin)
    second_bin = jnp.where(flipped == 1, left_bin, right_bin)
    return jnp.stack([first_bin, second_bin], axis=1).astype(jnp.int32)


def with_ends(entries, own_key, least, largest):
    longest = entries.shape.index(max(entries.shape))
    spots = []
    for shift in (0, 1):
        where = [jax.random.randint(jax.random.fold_in(own_key, axis), (), 0, length) for axis, length in enumerate(entries.shape)]
        where[longest] = (where[longest] + shift) % entries.shape[longest]
        spots.append(tuple(where))
    return entries.at[spots[0]].set(least).at[spots[1]].set(largest)


def gaussian(own_key, extent, deviation, limit, held_as=jnp.bfloat16):
    entries = deviation * jax.random.normal(own_key, extent, jnp.float32)
    return jnp.clip(entries, min=-limit, max=limit).astype(held_as)


def setup_inputs(seed: int = 0) -> dict:
    arg_keys = jax.random.split(jax.random.key(seed), 7)
    return {
        "lensing_maps": draw_lensing_maps(jax.random.fold_in(arg_keys[6], 71), 0),
        "filter_taps": gaussian(arg_keys[1], (SCALES, 2 * HALF + 1), (2 * HALF + 1) ** -0.5, 1.5, jnp.float32),
        "survey_mask": with_ends((jax.random.randint(arg_keys[2], (NX // 8, NY // 128), 0, 4) < 3).astype(jnp.int32), jax.random.fold_in(arg_keys[2], 1), 0, 1),
        "bin_pairs": draw_bin_pairs(jax.random.fold_in(arg_keys[6], 71), 0),
        "target_corr": gaussian(arg_keys[4], (PAIRS, SCALES, LAGS), 0.5, 3.0, jnp.float32),
        "pair_weight": jnp.clip(jnp.exp(jax.random.uniform(arg_keys[5], (PAIRS, SCALES, LAGS), jnp.float32, math.log(0.3), math.log(3.0))), 0.3, 3.0),
    }


HIGH = lax.Precision.HIGHEST


def expand_mask(survey_mask):
    values = survey_mask.astype(jnp.float32)
    tiles_x, tiles_y = values.shape
    return jnp.broadcast_to(values[:, None, :, None], (tiles_x, 8, tiles_y, 128)).reshape(tiles_x * 8, tiles_y * 128)


def smooth(haloed, filter_taps, row_count):
    tap_count = filter_taps.shape[1]
    half_width = (tap_count - 1) // 2
    widened = haloed.astype(jnp.float32)
    across = filter_taps[:, 0, None, None] * widened[None, 0:row_count]
    for a in range(1, tap_count):
        across = across + filter_taps[:, a, None, None] * widened[None, a:a + row_count]
    padded = jnp.pad(across, ((0, 0), (0, 0), (half_width, half_width)))
    col_count = widened.shape[1]
    result = filter_taps[:, 0, None, None] * padded[:, :, 0:col_count]
    for c in range(1, tap_count):
        result = result + filter_taps[:, c, None, None] * padded[:, :, c:c + col_count]
    return result.astype(jnp.bfloat16)


def lagged(left_maps, right_maps, pixmask, lag_count):
    col_count = left_maps.shape[2]
    columns = []
    for offset in range(lag_count):
        joint_mask = pixmask[:, :col_count - offset] * pixmask[:, offset:]
        product = left_maps[:, :, :col_count - offset].astype(jnp.float32) * right_maps[:, :, offset:].astype(jnp.float32) * joint_mask[None]
        columns.append(jnp.sum(product, axis=(1, 2)))
    return jnp.stack(columns, axis=1)


def adjoint_lags(partner, ahead_w, behind_w, pixmask):
    col_count = partner.shape[2]
    widened = partner.astype(jnp.float32)
    totals = jnp.zeros(partner.shape, jnp.float32)
    for offset in range(ahead_w.shape[1]):
        joint_mask = pixmask[:, :col_count - offset] * pixmask[:, offset:]
        front = jnp.pad(joint_mask[None] * widened[:, :, offset:], ((0, 0), (0, 0), (0, offset)))
        back = jnp.pad(joint_mask[None] * widened[:, :, :col_count - offset], ((0, 0), (0, 0), (offset, 0)))
        totals = totals + ahead_w[:, offset, None, None] * front + behind_w[:, offset, None, None] * back
    return totals


def adjoint_cols(grads, filter_taps):
    tap_count = filter_taps.shape[1]
    half_width = (tap_count - 1) // 2
    col_count = grads.shape[2]
    padded = jnp.pad(grads, ((0, 0), (0, 0), (half_width, half_width)))
    result = filter_taps[:, tap_count - 1, None, None] * padded[:, :, 0:col_count]
    for c in range(1, tap_count):
        result = result + filter_taps[:, tap_count - 1 - c, None, None] * padded[:, :, c:c + col_count]
    return result


def adjoint_rows(widened, filter_taps, row_count):
    tap_count = filter_taps.shape[1]
    result = filter_taps[:, tap_count - 1, None, None] * widened[:, 0:row_count]
    for a in range(1, tap_count):
        result = result + filter_taps[:, tap_count - 1 - a, None, None] * widened[:, a:a + row_count]
    return jnp.sum(result, axis=0)


def reference(lensing_maps, filter_taps, survey_mask, bin_pairs, target_corr, pair_weight):
    half_width = (filter_taps.shape[1] - 1) // 2
    pixmask = expand_mask(survey_mask)
    lag_count = pair_weight.shape[2]
    inverse_area = 1.0 / (NX * NY)

    def filter_one(one_map):
        return smooth(jnp.pad(one_map, ((half_width, half_width), (0, 0))), filter_taps, NX)

    filtered = lax.map(filter_one, lensing_maps)

    def row_of(left_maps):
        def with_partner(partner):
            return lagged(left_maps, partner, pixmask, lag_count) * inverse_area
        return lax.map(with_partner, filtered)

    pair_table = lax.map(row_of, filtered)
    indices = jnp.arange(BINS, dtype=jnp.int32)
    left_hot = (bin_pairs[:, 0:1] == indices[None, :]).astype(jnp.float32)
    right_hot = (bin_pairs[:, 1:2] == indices[None, :]).astype(jnp.float32)
    corr_table = jnp.einsum('pi,pj,ijsl->psl', left_hot, right_hot, pair_table, precision=HIGH)
    pair_grad = pair_weight * (corr_table - target_corr)
    table_grad = jnp.einsum('pi,pj,psl->ijsl', left_hot, right_hot, pair_grad, precision=HIGH)

    def grad_one(inputs):
        row_grad, col_grad = inputs

        def gather_term(totals, terms):
            partner, ahead_w, behind_w = terms
            return totals + adjoint_lags(partner, ahead_w, behind_w, pixmask), None

        totals, _ = lax.scan(gather_term, jnp.zeros((SCALES, NX, NY), jnp.float32), (filtered, row_grad, col_grad))
        col_pass = adjoint_cols(totals, filter_taps)
        widened = jnp.pad(col_pass, ((0, 0), (half_width, half_width), (0, 0)))
        return adjoint_rows(widened, filter_taps, NX)

    map_gradient = lax.map(grad_one, (table_grad, jnp.transpose(table_grad, (1, 0, 2, 3))))
    return (corr_table, map_gradient)
```

```python
import functools

import jax
import jax.numpy as jnp
from jax import lax
from jax.experimental import pallas as pl
from jax.experimental.pallas import tpu as pltpu
from jax.sharding import PartitionSpec as P

HIGH = lax.Precision.HIGHEST
F32 = jnp.float32
BF16 = jnp.bfloat16
XB = 32
MESH = pl.DeviceIdType.MESH
VMEM_LIMIT = 60 * 1024 * 1024


def round_up(n, m):
    return -(-n // m) * m


def halves(value):
    hi = value.astype(BF16)
    lo = (value - hi.astype(F32)).astype(BF16)
    return hi, lo


def outer_halves(value):
    hi = lax.reduce_precision(value, exponent_bits=8, mantissa_bits=7)
    return hi.astype(BF16), (value - hi).astype(BF16)


def mm(a, b):
    return jnp.dot(a, b, preferred_element_type=F32)


def mm3(a, b):
    return mm(a[0], b[0]) + mm(a[0], b[1]) + mm(a[1], b[0])


def place(bins, sky):
    return lax.axis_index("bin") * sky + lax.axis_index("sky")


def greet(me, bins, sky):
    count = bins * sky
    barrier = pltpu.get_barrier_semaphore()

    def hello(k, carry):
        other = lax.rem(me + k, count)
        pl.semaphore_signal(
            barrier, inc=1, device_id=(other // sky, lax.rem(other, sky)), device_id_type=MESH
        )
        return carry

    lax.fori_loop(1, count, hello, 0)
    pl.semaphore_wait(barrier, count - 1)


def exchange_kernel(bins, sky, dst_of, x_ref, y_ref, send_sem, recv_sem, own_sem):
    count = bins * sky
    me = place(bins, sky)
    greet(me, bins, sky)

    def copy_to(other):
        return pltpu.make_async_remote_copy(
            src_ref=x_ref.at[other],
            dst_ref=dst_of(y_ref, me),
            send_sem=send_sem.at[other],
            recv_sem=recv_sem.at[me],
            device_id=(other // sky, lax.rem(other, sky)),
            device_id_type=MESH,
        )

    def start(k, carry):
        copy_to(lax.rem(me + k, count)).start()
        return carry

    lax.fori_loop(1, count, start, 0)
    own = pltpu.make_async_copy(x_ref.at[me], dst_of(y_ref, me), own_sem)
    own.start()

    def finish(k, carry):
        other = lax.rem(me + count - k, count)
        pltpu.make_async_remote_copy(
            src_ref=x_ref.at[other],
            dst_ref=dst_of(y_ref, other),
            send_sem=send_sem.at[other],
            recv_sem=recv_sem.at[other],
            device_id=(other // sky, lax.rem(other, sky)),
            device_id_type=MESH,
        ).wait()
        return carry

    lax.fori_loop(1, count, finish, 0)
    own.wait()


def exchange(x, bins, sky, out_shape, dst_of, collective_id):
    count = bins * sky
    return pl.pallas_call(
        functools.partial(exchange_kernel, bins, sky, dst_of),
        out_shape=jax.ShapeDtypeStruct(out_shape, x.dtype),
        in_specs=[pl.BlockSpec(memory_space=pltpu.VMEM)],
        out_specs=pl.BlockSpec(memory_space=pltpu.VMEM),
        scratch_shapes=[
            pltpu.SemaphoreType.DMA((count,)),
            pltpu.SemaphoreType.DMA((count,)),
            pltpu.SemaphoreType.DMA,
        ],
        compiler_params=pltpu.CompilerParams(
            collective_id=collective_id, has_side_effects=True, vmem_limit_bytes=VMEM_LIMIT
        ),
    )(x)


def total_kernel(bins, sky, x_ref, y_ref, slots, send_sem, recv_sem):
    count = bins * sky
    me = place(bins, sky)
    greet(me, bins, sky)

    def copy_for(other, slot):
        return pltpu.make_async_remote_copy(
            src_ref=x_ref,
            dst_ref=slots.at[slot],
            send_sem=send_sem.at[other],
            recv_sem=recv_sem.at[slot],
            device_id=(other // sky, lax.rem(other, sky)),
            device_id_type=MESH,
        )

    def start(k, carry):
        copy_for(lax.rem(me + k, count), me).start()
        return carry

    lax.fori_loop(1, count, start, 0)
    slots[pl.ds(me, 1)] = x_ref[...][None]

    def finish(k, carry):
        other = lax.rem(me + count - k, count)
        copy_for(other, other).wait()
        return carry

    lax.fori_loop(1, count, finish, 0)
    y_ref[...] = lax.fori_loop(
        1, count, lambda k, acc: acc + slots[k], slots[0]
    )


def total(x, bins, sky, collective_id):
    count = bins * sky
    return pl.pallas_call(
        functools.partial(total_kernel, bins, sky),
        out_shape=jax.ShapeDtypeStruct(x.shape, x.dtype),
        in_specs=[pl.BlockSpec(memory_space=pltpu.VMEM)],
        out_specs=pl.BlockSpec(memory_space=pltpu.VMEM),
        scratch_shapes=[
            pltpu.VMEM((count,) + x.shape, x.dtype),
            pltpu.SemaphoreType.DMA((count,)),
            pltpu.SemaphoreType.DMA((count,)),
        ],
        compiler_params=pltpu.CompilerParams(collective_id=collective_id, has_side_effects=True),
    )(x)


def col_matrix(row, width, shift, out_width):
    full = pltpu.roll(
        jnp.broadcast_to(row, (width, width)), shift % width, 1, stride=1, stride_axis=0
    )
    return halves(full[:, :out_width])


def window_mask(y_ref, group, bins, sky, chunk, halo, width, tiles):
    rows = y_ref[0, pl.ds(group * XB, XB), :].astype(F32)
    me = place(bins, sky)
    start = me * chunk - halo + 128 * tiles
    lanes = lax.broadcasted_iota(jnp.int32, (XB, width), 1)
    which = (lanes + start) // 128 - start // 128
    mask = jnp.zeros((XB, width), F32)
    for t in range(tiles):
        value = jnp.broadcast_to(rows[:, t : t + 1], (XB, width))
        mask = jnp.where(which == t, value, mask)
    return mask


def same_row(count):
    left = lax.rem(lax.broadcasted_iota(jnp.int32, (count, count), 0), XB)
    right = lax.rem(lax.broadcasted_iota(jnp.int32, (count, count), 1), XB)
    return (left == right).astype(F32)


def forward_kernel(
    bins, sky, scales, lags, groups, chunk, halo, tiles,
    y_ref, row_ref, tap_ref, g_ref, table_ref, hi_ref, lo_ref, sums_ref,
):
    width = y_ref.shape[2]
    size = bins * XB
    rows = groups * XB

    for b in range(bins):
        y = y_ref[b]
        passed = mm(row_ref[...], jnp.concatenate([y, y, y], axis=0))
        hi, lo = halves(passed)
        for s in range(scales):
            for g in range(groups):
                part = slice(s * rows + g * XB, s * rows + (g + 1) * XB)
                hi_ref[s * groups + g, b * XB : (b + 1) * XB, :] = hi[part]
                lo_ref[s * groups + g, b * XB : (b + 1) * XB, :] = lo[part]

    sums_ref[...] = jnp.zeros_like(sums_ref)
    diag = same_row(size)
    lanes = lax.broadcasted_iota(jnp.int32, (size, width), 1)
    owned = (lanes >= halo) & (lanes < halo + chunk)

    def one(step, carry):
        s, g = step // groups, lax.rem(step, groups)
        matrix = col_matrix(tap_ref[s], width, width - 8, width)
        mask = window_mask(y_ref, g, bins, sky, chunk, halo, width, tiles)
        filtered = mm3((hi_ref[step], lo_ref[step]), matrix).astype(BF16).astype(F32)
        kept = jnp.where(jnp.concatenate([mask] * bins, axis=0) > 0, filtered, 0.0)
        g_ref[step] = kept.astype(BF16)
        left = jnp.where(owned, kept, 0.0).astype(BF16)
        for l in range(lags):
            right = kept if l == 0 else pltpu.roll(kept, width - l, 1)
            gram = lax.dot_general(
                left, right.astype(BF16), (((1,), (1,)), ((), ())), preferred_element_type=F32
            )
            gram = jnp.sum((gram * diag).reshape(bins, XB, size), axis=1)
            at = s * lags + l
            sums_ref[at] = sums_ref[at] + gram
        return carry

    lax.fori_loop(0, scales * groups, one, 0)
    spot = lax.rem(lax.broadcasted_iota(jnp.int32, (bins, size), 1), XB)
    table = jnp.zeros((bins, size), F32)
    for at in range(scales * lags):
        value = sums_ref[at]
        for step in (16, 8, 4, 2, 1):
            value = value + pltpu.roll(value, size - step, 1)
        if at:
            value = pltpu.roll(value, at, 1)
        table = jnp.where(spot == at, value, table)
    table_ref[...] = table


def backward_kernel(
    bins, sky, scales, lags, groups, chunk, halo, tiles,
    y_ref, g_ref, coef_ref, row_ref, tap_ref, out_ref, hi_ref, lo_ref,
):
    width = y_ref.shape[2]
    out_width = out_ref.shape[2]
    size = bins * XB
    rows = groups * XB
    shifts = 2 * lags - 1
    diag = same_row(size)

    def one(step, carry):
        s, g = step // groups, lax.rem(step, groups)
        matrix = col_matrix(tap_ref[s], width, width - 8 - halo, out_width)
        mask = window_mask(y_ref, g, bins, sky, chunk, halo, width, tiles)
        maps = g_ref[step].astype(F32)
        total_grad = jnp.zeros((size, width), F32)
        for d in range(shifts):
            shift = d - (lags - 1)
            moved = maps if shift == 0 else pltpu.roll(maps, (width - shift) % width, 1)
            moved = moved.astype(BF16)
            coef = coef_ref[s * shifts + d]
            spread = jnp.broadcast_to(coef[:, None, :], (bins, XB, size)).reshape(size, size)
            hi, lo = halves(spread * diag)
            total_grad = total_grad + mm(hi, moved) + mm(lo, moved)
        total_grad = jnp.where(jnp.concatenate([mask] * bins, axis=0) > 0, total_grad, 0.0)
        hi, lo = halves(mm3(halves(total_grad), matrix))
        hi_ref[step] = hi
        lo_ref[step] = lo
        return carry

    lax.fori_loop(0, scales * groups, one, 0)
    for b in range(bins):
        hi = jnp.concatenate(
            [hi_ref[k, b * XB : (b + 1) * XB, :] for k in range(scales * groups)], axis=0
        )
        lo = jnp.concatenate(
            [lo_ref[k, b * XB : (b + 1) * XB, :] for k in range(scales * groups)], axis=0
        )
        out_ref[b] = mm3((row_ref[0], row_ref[1]), (hi, lo))


def vmem_call(kernel, out_shape, scratch, inputs):
    spec = pl.BlockSpec(memory_space=pltpu.VMEM)
    return pl.pallas_call(
        kernel,
        out_shape=out_shape,
        in_specs=[spec] * len(inputs),
        out_specs=jax.tree.map(lambda _: spec, out_shape),
        scratch_shapes=scratch,
        compiler_params=pltpu.CompilerParams(vmem_limit_bytes=VMEM_LIMIT),
    )(*inputs)


def per_device(lensing_maps, filter_taps, survey_mask, bin_pairs, target_corr, pair_weight):
    scales, tap_count = filter_taps.shape
    half = (tap_count - 1) // 2
    strip = lensing_maps[0]
    strip_rows, cols = strip.shape
    bins, sky = lax.axis_size("bin"), lax.axis_size("sky")
    count = bins * sky
    lags = pair_weight.shape[2]
    row_count = strip_rows * sky
    groups = row_count // XB
    chunk = cols // count
    width = round_up(chunk + 2 * (2 * half + lags - 1), 128)
    halo = (width - chunk) // 2
    out_width = round_up(chunk, 128)
    tiles = width // 128 + 1
    size = bins * XB

    padded = jnp.pad(strip, ((0, 0), (halo, halo)))
    windows = jnp.stack([padded[:, d * chunk : d * chunk + width] for d in range(count)])
    first = [(d * chunk - halo) // 128 for d in range(count)]
    low = -min(first)
    tile_row = jnp.pad(survey_mask[0].astype(BF16), (low, tiles))
    marks = jnp.stack([tile_row[f + low : f + low + tiles] for f in first])
    marks = jnp.pad(marks, ((0, 0), (0, width - tiles)))[:, None, :]
    lanes = lax.broadcasted_iota(jnp.int32, windows.shape, 2)
    windows = jnp.where(lanes < tiles, marks, windows)

    offset = jnp.arange(row_count)[None, :] - jnp.arange(row_count)[:, None] + half
    row_matrix = jnp.zeros((scales, row_count, row_count), F32)
    for a in range(tap_count):
        row_matrix = jnp.where(offset[None] == a, filter_taps[:, a, None, None], row_matrix)
    flat = row_matrix.reshape(scales * row_count, row_count)
    hi = lax.reduce_precision(flat, exponent_bits=8, mantissa_bits=7)
    row_forward = jnp.concatenate([hi.astype(BF16), *outer_halves(flat - hi)], axis=1)
    back = jnp.transpose(row_matrix, (2, 0, 1)).reshape(row_count, scales * row_count)
    row_backward = jnp.stack(outer_halves(back))
    wide = jnp.pad(filter_taps, ((0, 0), (0, width - tap_count)))[:, None, :]
    wide_rev = jnp.pad(filter_taps[:, ::-1], ((0, 0), (0, width - tap_count)))[:, None, :]

    index = jnp.arange(bins * bins, dtype=jnp.int32)
    hot = (bin_pairs[:, 0:1] * bins + bin_pairs[:, 1:2] == index[None, :]).astype(F32)
    both = jnp.concatenate(
        [pair_weight.reshape(-1, scales * lags), target_corr.reshape(-1, scales * lags)], axis=1
    )
    dense = jnp.einsum("pk,pn->kn", hot, both, precision=HIGH)
    weight, target = dense[:, : scales * lags], dense[:, scales * lags :]

    received = exchange(
        windows, bins, sky, (count, strip_rows, width), lambda ref, d: ref.at[d], 1
    )
    maps = received.reshape(bins, row_count, width)

    settings = (bins, sky, scales, lags, groups, chunk, halo, tiles)
    kept, sums = vmem_call(
        functools.partial(forward_kernel, *settings),
        (
            jax.ShapeDtypeStruct((scales * groups, size, width), BF16),
            jax.ShapeDtypeStruct((bins, size), F32),
        ),
        [
            pltpu.VMEM((scales * groups, size, width), BF16),
            pltpu.VMEM((scales * groups, size, width), BF16),
            pltpu.VMEM((scales * lags, bins, size), F32),
        ],
        (maps, row_forward, wide_rev),
    )
    sums = total(sums, bins, sky, 2)
    table = sums.reshape(bins * bins, XB)[:, : scales * lags] * (1.0 / (row_count * cols))
    corr_table = jnp.einsum("pk,kn->pn", hot, table, precision=HIGH).reshape(-1, scales, lags)

    grad = (weight * (table - target)).reshape(bins, bins, scales, lags)
    turned = jnp.transpose(grad, (1, 0, 2, 3))
    coefs = []
    for d in range(1 - lags, lags):
        if d == 0:
            coefs.append(grad[..., 0] + turned[..., 0])
        else:
            coefs.append(grad[..., d] if d > 0 else turned[..., -d])
    coef = jnp.transpose(jnp.stack(coefs), (3, 0, 1, 2))
    coef = jnp.broadcast_to(coef[..., None], coef.shape + (XB,))
    coef = coef.reshape(scales * (2 * lags - 1), bins, size)

    gradient = vmem_call(
        functools.partial(backward_kernel, *settings),
        jax.ShapeDtypeStruct((bins, row_count, out_width), F32),
        [
            pltpu.VMEM((scales * groups, size, out_width), BF16),
            pltpu.VMEM((scales * groups, size, out_width), BF16),
        ],
        (maps, kept, coef, row_backward, wide),
    )
    outgoing = gradient.reshape(count, strip_rows, out_width)
    if chunk == out_width:
        result = exchange(
            outgoing, bins, sky, (strip_rows, cols),
            lambda ref, d: ref.at[:, pl.ds(pl.multiple_of(d * chunk, 128), chunk)], 3,
        )
    else:
        parts = exchange(
            outgoing, bins, sky, (count, strip_rows, out_width), lambda ref, d: ref.at[d], 3
        )
        result = jnp.transpose(parts[:, :, :chunk], (1, 0, 2)).reshape(strip_rows, cols)
    return (corr_table, result[None])


def solution(mesh):
    placed = (P("bin", "sky", None), P(), P("sky", None), P(), P(), P())
    return jax.shard_map(
        per_device,
        mesh=mesh,
        in_specs=placed,
        out_specs=(P(), P("bin", "sky", None)),
        check_vma=False,
    )
```

```python
import functools

import jax
import jax.numpy as jnp
from jax import lax
from jax.experimental import pallas as pl
from jax.experimental.pallas import tpu as pltpu
from jax.sharding import PartitionSpec as P

F32 = jnp.float32
BF16 = jnp.bfloat16
XB = 32
MESH = pl.DeviceIdType.MESH
VMEM_LIMIT = 60 * 1024 * 1024


def round_up(n, m):
    return -(-n // m) * m


def halves(value):
    hi = value.astype(BF16)
    lo = (value - hi.astype(F32)).astype(BF16)
    return hi, lo


def mm(a, b):
    return jnp.dot(a, b, preferred_element_type=F32)


def mm3(a, b):
    return mm(a[0], b[0]) + mm(a[0], b[1]) + mm(a[1], b[0])


def place(bins, sky):
    return lax.axis_index("bin") * sky + lax.axis_index("sky")


def greet(me, bins, sky):
    count = bins * sky
    barrier = pltpu.get_barrier_semaphore()

    def hello(k, carry):
        other = lax.rem(me + k, count)
        pl.semaphore_signal(
            barrier, inc=1, device_id=(other // sky, lax.rem(other, sky)), device_id_type=MESH
        )
        return carry

    lax.fori_loop(1, count, hello, 0)
    pl.semaphore_wait(barrier, count - 1)


def band(row, height, width, shift, out_width):
    full = pltpu.roll(
        jnp.broadcast_to(row, (height, width)), width - shift, 1, stride=1, stride_axis=0
    )
    return full[:, :out_width]


def same_row(count):
    left = lax.rem(lax.broadcasted_iota(jnp.int32, (count, count), 0), XB)
    right = lax.rem(lax.broadcasted_iota(jnp.int32, (count, count), 1), XB)
    return (left == right).astype(F32)


def step_kernel(
    bins, sky, scales, lags, groups, chunk, halo, tiles, half, area, src_of, dst_of,
    x_ref, mark_ref, tap_ref, pair_ref, fit_ref,
    result_ref, corr_ref,
    y_ref, marks_ref, hi_ref, lo_ref, g_ref, sums_ref, grad_ref,
    col_ref, adj_ref, part_ref, sky_ref, bin_in_ref, bin_ref,
    send_x, recv_x, send_m, recv_m, send_s, recv_s, send_b, recv_b, send_g, recv_g, own_sem,
):
    count = bins * sky
    strip_rows, width = y_ref.shape[1], y_ref.shape[2]
    out_width = grad_ref.shape[2]
    size = bins * XB
    rows = groups * XB
    my_bin, my_sky = lax.axis_index("bin"), lax.axis_index("sky")
    me = place(bins, sky)
    greet(me, bins, sky)

    def window_copy(other, slot):
        return pltpu.make_async_remote_copy(
            src_ref=src_of(x_ref, other),
            dst_ref=y_ref.at[slot],
            send_sem=send_x.at[other],
            recv_sem=recv_x.at[slot],
            device_id=(other // sky, lax.rem(other, sky)),
            device_id_type=MESH,
        )

    def along(axis, src, dst, send, recv, other, slot):
        return pltpu.make_async_remote_copy(
            src_ref=src,
            dst_ref=dst.at[slot],
            send_sem=send.at[other],
            recv_sem=recv.at[slot],
            device_id=(my_bin, other) if axis == "sky" else (other, my_sky),
            device_id_type=MESH,
        )

    def each(n, mine, act):
        def body(k, carry):
            act(lax.rem(mine + k, n))
            return carry

        lax.fori_loop(1, n, body, 0)

    each(sky, my_sky, lambda o: along("sky", mark_ref, marks_ref, send_m, recv_m, o, my_sky).start())
    each(count, me, lambda o: window_copy(o, me).start())
    own_mark = pltpu.make_async_copy(mark_ref, marks_ref.at[my_sky], own_sem.at[0])
    own_mark.start()
    own = pltpu.make_async_copy(src_of(x_ref, me), y_ref.at[me], own_sem.at[1])
    own.start()

    tall = tap_ref.shape[3]
    row_hi, row_lo, back_hi, back_lo = [], [], [], []
    narrow = round_up(rows + 2 * half + 1, 128)
    for s in range(scales):
        taps, turned = tap_ref[0, s], tap_ref[1, s]
        for at, part in enumerate(halves(band(turned[:, :width], width, width, half, width))):
            col_ref[at, s] = part
        for at, part in enumerate(
            halves(band(taps[:, :width], width, width, half + halo, out_width))
        ):
            adj_ref[at, s] = part
        a, b = halves(band(taps[:, :narrow], rows, narrow, half, rows))
        row_hi.append(a)
        row_lo.append(b)
        back = band(turned[:, :narrow], rows, narrow, half, rows)
        back_hi.append(back)
    row_hi = jnp.concatenate(row_hi, axis=0)
    row_lo = jnp.concatenate(row_lo, axis=0)
    back = halves(jnp.concatenate(back_hi, axis=1))
    diag = same_row(size)
    lanes = lax.broadcasted_iota(jnp.int32, (size, width), 1)
    owned = (lanes >= halo) & (lanes < halo + chunk)
    spot = lax.rem(lax.broadcasted_iota(jnp.int32, (bins, size), 1), XB)
    bin_row = lax.broadcasted_iota(jnp.int32, (bins, size), 0)

    pairs = fit_ref.shape[1]
    first = jnp.broadcast_to(pair_ref[:, 0:1], (pairs, size))
    second = jnp.broadcast_to(pair_ref[:, 1:2], (pairs, size))
    right_hot = lax.broadcasted_iota(jnp.int32, (pairs, size), 1) // XB == second
    weight = jnp.zeros((bins, size), F32)
    target = jnp.zeros((bins, size), F32)
    for i in range(bins):
        hot = right_hot & (first == i)
        weight_row = jnp.sum(jnp.where(hot, fit_ref[0], 0.0), axis=0, keepdims=True)
        target_row = jnp.sum(jnp.where(hot, fit_ref[1], 0.0), axis=0, keepdims=True)
        weight = jnp.where(bin_row == i, weight_row, weight)
        target = jnp.where(bin_row == i, target_row, target)
    sums_ref[...] = jnp.zeros_like(sums_ref)

    each(sky, my_sky, lambda o: along("sky", mark_ref, marks_ref, send_m, recv_m, o, o).wait())
    own_mark.wait()
    each(count, me, lambda o: window_copy(o, o).wait())
    own.wait()

    mark_width = mark_ref.shape[1]
    start = me * chunk - halo + 128
    marks = marks_ref[...].reshape(rows, mark_width)
    marks = pltpu.roll(marks, lax.rem(mark_width - start // 128, mark_width), 1)
    which = (lax.broadcasted_iota(jnp.int32, (rows, width), 1) + start) // 128 - start // 128
    mask = jnp.zeros((rows, width), F32)
    for t in range(tiles):
        mask = jnp.where(which == t, jnp.broadcast_to(marks[:, t : t + 1], (rows, width)), mask)
    masks = [
        jnp.concatenate([mask[g * XB : (g + 1) * XB]] * bins, axis=0) > 0 for g in range(groups)
    ]

    for b in range(bins):
        y = jnp.concatenate([y_ref[b * sky + k].astype(F32) for k in range(sky)], axis=0)
        y = y.astype(BF16)
        hi, lo = halves(mm(row_hi, y) + mm(row_lo, y))
        for s in range(scales):
            for g in range(groups):
                part = slice(s * rows + g * XB, s * rows + (g + 1) * XB)
                hi_ref[g, s, b * XB : (b + 1) * XB, :] = hi[part]
                lo_ref[g, s, b * XB : (b + 1) * XB, :] = lo[part]

    for g in range(groups):

        def forward(s, carry):
            matrix = (col_ref[0, s], col_ref[1, s])
            filtered = mm3((hi_ref[g, s], lo_ref[g, s]), matrix).astype(BF16).astype(F32)
            kept = jnp.where(masks[g], filtered, 0.0)
            g_ref[g, s] = kept.astype(BF16)
            left = jnp.where(owned, kept, 0.0).astype(BF16)
            for l in range(lags):
                right = kept if l == 0 else pltpu.roll(kept, width - l, 1)
                gram = lax.dot_general(
                    left, right.astype(BF16), (((1,), (1,)), ((), ())), preferred_element_type=F32
                )
                gram = jnp.sum((gram * diag).reshape(bins, XB, size), axis=1)
                sums_ref[s * lags + l] = sums_ref[s * lags + l] + gram
            return carry

        lax.fori_loop(0, scales, forward, 0)

    table = jnp.zeros((bins, size), F32)
    for at in range(scales * lags):
        value = sums_ref[at]
        for step in (16, 8, 4, 2, 1):
            value = value + pltpu.roll(value, size - step, 1)
        if at:
            value = pltpu.roll(value, at, 1)
        table = jnp.where(spot == at, value, table)

    part_ref[...] = table
    each(sky, my_sky, lambda o: along("sky", part_ref, sky_ref, send_s, recv_s, o, my_sky).start())
    sky_ref[pl.ds(my_sky, 1)] = table[None]
    each(sky, my_sky, lambda o: along("sky", part_ref, sky_ref, send_s, recv_s, o, o).wait())
    table = sky_ref[0]
    for k in range(1, sky):
        table = table + sky_ref[k]
    bin_in_ref[...] = table
    each(bins, my_bin, lambda o: along("bin", bin_in_ref, bin_ref, send_b, recv_b, o, my_bin).start())
    bin_ref[pl.ds(my_bin, 1)] = table[None]
    each(bins, my_bin, lambda o: along("bin", bin_in_ref, bin_ref, send_b, recv_b, o, o).wait())
    table = bin_ref[0]
    for k in range(1, bins):
        table = table + bin_ref[k]
    table = table * area

    picked = jnp.zeros((pairs, size), F32)
    for i in range(bins):
        picked = jnp.where(first == i, jnp.broadcast_to(table[i : i + 1], (pairs, size)), picked)
    picked = jnp.where(right_hot, picked, 0.0)
    step = size // 2
    while step >= XB:
        picked = picked + pltpu.roll(picked, step, 1)
        step //= 2
    corr_ref[...] = picked

    ahead = jnp.where(spot < scales * lags, weight * (table - target), 0.0)
    spread = jnp.broadcast_to(ahead[:, None, :], (bins, XB, size)).reshape(size, size)
    behind = jnp.sum(jnp.transpose(spread * diag).reshape(bins, XB, size), axis=1)

    def coefficient(values, at):
        value = jnp.where(spot == at, values, 0.0)
        value = pltpu.roll(value, lax.rem(size - at, size), 1)
        for step in (1, 2, 4, 8, 16):
            value = value + pltpu.roll(value, step, 1)
        return value

    for g in range(groups):

        def backward(s, carry):
            maps = g_ref[g, s].astype(F32)
            total_grad = jnp.zeros((size, width), F32)
            for shift in range(1 - lags, lags):
                moved = maps if shift == 0 else pltpu.roll(maps, (width - shift) % width, 1)
                moved = moved.astype(BF16)
                if shift == 0:
                    coef = coefficient(ahead + behind, s * lags)
                elif shift > 0:
                    coef = coefficient(ahead, s * lags + shift)
                else:
                    coef = coefficient(behind, s * lags - shift)
                full = jnp.broadcast_to(coef[:, None, :], (bins, XB, size)).reshape(size, size)
                hi, lo = halves(full * diag)
                total_grad = total_grad + mm(hi, moved) + mm(lo, moved)
            total_grad = jnp.where(masks[g], total_grad, 0.0)
            hi, lo = halves(mm3(halves(total_grad), (adj_ref[0, s], adj_ref[1, s])))
            hi_ref[g, s, :, :out_width] = hi
            lo_ref[g, s, :, :out_width] = lo
            return carry

        lax.fori_loop(0, scales, backward, 0)

    for b in range(bins):
        spots = [(g, s) for s in range(scales) for g in range(groups)]
        rows_of = slice(b * XB, (b + 1) * XB)
        hi = jnp.concatenate([hi_ref[g, s, rows_of, :out_width] for g, s in spots], axis=0)
        lo = jnp.concatenate([lo_ref[g, s, rows_of, :out_width] for g, s in spots], axis=0)
        total_rows = mm3(back, (hi, lo))
        for k in range(sky):
            grad_ref[b * sky + k] = total_rows[k * strip_rows : (k + 1) * strip_rows]

    def grad_copy(other, slot):
        return pltpu.make_async_remote_copy(
            src_ref=grad_ref.at[other],
            dst_ref=dst_of(result_ref, slot),
            send_sem=send_g.at[other],
            recv_sem=recv_g.at[slot],
            device_id=(other // sky, lax.rem(other, sky)),
            device_id_type=MESH,
        )

    each(count, me, lambda o: grad_copy(o, me).start())
    own_grad = pltpu.make_async_copy(grad_ref.at[me], dst_of(result_ref, me), own_sem.at[2])
    own_grad.start()
    each(count, me, lambda o: grad_copy(o, o).wait())
    own_grad.wait()


def per_device(lensing_maps, filter_taps, survey_mask, bin_pairs, target_corr, pair_weight):
    scales, tap_count = filter_taps.shape
    half = (tap_count - 1) // 2
    strip = lensing_maps[0]
    strip_rows, cols = strip.shape
    bins, sky = lax.axis_size("bin"), lax.axis_size("sky")
    count = bins * sky
    pairs, lags = pair_weight.shape[0], pair_weight.shape[2]
    row_count = strip_rows * sky
    groups = row_count // XB
    chunk = cols // count
    width = round_up(chunk + 2 * (2 * half + lags - 1), 128)
    halo = (width - chunk) // 2
    out_width = round_up(chunk, 128)
    tiles = width // 128 + 1
    size = bins * XB
    aligned = chunk % 128 == 0

    windows = jnp.pad(strip, ((0, 0), (halo, halo)))
    if not aligned:
        windows = jnp.stack([windows[:, d * chunk : d * chunk + width] for d in range(count)])
    mark_width = round_up(survey_mask.shape[1] + 1 + tiles, 128)
    marks = jnp.pad(
        survey_mask.astype(F32), ((0, 0), (1, mark_width - survey_mask.shape[1] - 1))
    )
    marks = jnp.broadcast_to(marks, (strip_rows, mark_width))
    tall = max(width, round_up(row_count + 2 * half + 1, 128))
    taps = jnp.stack([filter_taps, filter_taps[:, ::-1]])
    taps = jnp.pad(taps, ((0, 0), (0, 0), (0, tall - tap_count)))[:, :, None, :]
    fit = jnp.stack([pair_weight, target_corr]).reshape(2, pairs, scales * lags)
    fit = jnp.tile(jnp.pad(fit, ((0, 0), (0, 0), (0, XB - scales * lags))), (1, 1, bins))

    if aligned:
        src_of = lambda ref, d: ref.at[:, pl.ds(pl.multiple_of(d * chunk, 128), width)]
        dst_of = lambda ref, d: ref.at[:, pl.ds(pl.multiple_of(d * chunk, 128), chunk)]
        result_shape = (strip_rows, cols)
    else:
        src_of = lambda ref, d: ref.at[d]
        dst_of = lambda ref, d: ref.at[d]
        result_shape = (count, strip_rows, out_width)

    spec = pl.BlockSpec(memory_space=pltpu.VMEM)
    table_shape = (bins, size)
    dma = pltpu.SemaphoreType.DMA
    result, corr = pl.pallas_call(
        functools.partial(
            step_kernel, bins, sky, scales, lags, groups, chunk, halo, tiles, half,
            1.0 / (row_count * cols), src_of, dst_of,
        ),
        out_shape=(
            jax.ShapeDtypeStruct(result_shape, F32),
            jax.ShapeDtypeStruct((pairs, size), F32),
        ),
        in_specs=[spec] * 5,
        out_specs=(spec, spec),
        scratch_shapes=[
            pltpu.VMEM((count, strip_rows, width), BF16),
            pltpu.VMEM((sky, strip_rows, mark_width), F32),
            pltpu.VMEM((groups, scales, size, width), BF16),
            pltpu.VMEM((groups, scales, size, width), BF16),
            pltpu.VMEM((groups, scales, size, width), BF16),
            pltpu.VMEM((scales * lags,) + table_shape, F32),
            pltpu.VMEM((count, strip_rows, out_width), F32),
            pltpu.VMEM((2, scales, width, width), BF16),
            pltpu.VMEM((2, scales, width, out_width), BF16),
            pltpu.VMEM(table_shape, F32),
            pltpu.VMEM((sky,) + table_shape, F32),
            pltpu.VMEM(table_shape, F32),
            pltpu.VMEM((bins,) + table_shape, F32),
            dma((count,)), dma((count,)), dma((sky,)), dma((sky,)), dma((sky,)), dma((sky,)),
            dma((bins,)), dma((bins,)), dma((count,)), dma((count,)), dma((3,)),
        ],
        compiler_params=pltpu.CompilerParams(
            collective_id=1, has_side_effects=True, vmem_limit_bytes=VMEM_LIMIT
        ),
    )(windows, marks, taps, bin_pairs, fit)
    if not aligned:
        result = jnp.transpose(result[:, :, :chunk], (1, 0, 2)).reshape(strip_rows, cols)
    corr_table = corr[:, : scales * lags].reshape(pairs, scales, lags)
    return (corr_table, result[None])


def solution(mesh):
    placed = (P("bin", "sky", None), P(), P("sky", None), P(), P(), P())
    return jax.shard_map(
        per_device,
        mesh=mesh,
        in_specs=placed,
        out_specs=(P(), P("bin", "sky", None)),
        check_vma=False,
    )
```

```python
import functools

import jax
import jax.numpy as jnp
from jax import lax
from jax.experimental import pallas as pl
from jax.experimental.pallas import tpu as pltpu
from jax.sharding import PartitionSpec as P

F32 = jnp.float32
BF16 = jnp.bfloat16
XB = 32
MESH = pl.DeviceIdType.MESH
VMEM_LIMIT = 60 * 1024 * 1024


def round_up(n, m):
    return -(-n // m) * m


def halves(value):
    hi = value.astype(BF16)
    lo = (value - hi.astype(F32)).astype(BF16)
    return hi, lo


def mm(a, b):
    return jnp.dot(a, b, preferred_element_type=F32)


def mm3(a, b):
    return mm(a[0], b[0]) + mm(a[0], b[1]) + mm(a[1], b[0])


def place(bins, sky):
    return lax.axis_index("bin") * sky + lax.axis_index("sky")


def greet(me, bins, sky):
    count = bins * sky
    barrier = pltpu.get_barrier_semaphore()

    def hello(k, carry):
        other = lax.rem(me + k, count)
        pl.semaphore_signal(
            barrier, inc=1, device_id=(other // sky, lax.rem(other, sky)), device_id_type=MESH
        )
        return carry

    lax.fori_loop(1, count, hello, 0)
    pl.semaphore_wait(barrier, count - 1)


def band(row, height, width, shift, out_width):
    full = pltpu.roll(
        jnp.broadcast_to(row, (height, width)), width - shift, 1, stride=1, stride_axis=0
    )
    return full[:, :out_width]


def same_row(count):
    left = lax.rem(lax.broadcasted_iota(jnp.int32, (count, count), 0), XB)
    right = lax.rem(lax.broadcasted_iota(jnp.int32, (count, count), 1), XB)
    return (left == right).astype(F32)


def step_kernel(
    bins, sky, scales, lags, groups, chunk, halo, tiles, half, area, src_of, dst_of,
    x_ref, mark_ref, tap_ref, pair_ref, fit_ref,
    result_ref, corr_ref,
    y_ref, marks_ref, hi_ref, lo_ref, g_ref, sums_ref, grad_ref,
    col_ref, adj_ref, part_ref, sky_ref, bin_in_ref, bin_ref,
    send_x, recv_x, send_m, recv_m, send_s, recv_s, send_b, recv_b, send_g, recv_g, own_sem, coef_ref,
):
    count = bins * sky
    strip_rows, width = y_ref.shape[1], y_ref.shape[2]
    pieces, part_width = grad_ref.shape[0], grad_ref.shape[3]
    span = adj_ref.shape[2]
    size = bins * XB
    rows = groups * XB
    my_bin, my_sky = lax.axis_index("bin"), lax.axis_index("sky")
    me = place(bins, sky)
    greet(me, bins, sky)

    def window_copy(other, slot):
        return pltpu.make_async_remote_copy(
            src_ref=src_of(x_ref, other),
            dst_ref=y_ref.at[slot],
            send_sem=send_x.at[other],
            recv_sem=recv_x.at[slot],
            device_id=(other // sky, lax.rem(other, sky)),
            device_id_type=MESH,
        )

    def along(axis, src, dst, send, recv, other, slot):
        return pltpu.make_async_remote_copy(
            src_ref=src,
            dst_ref=dst.at[slot],
            send_sem=send.at[other],
            recv_sem=recv.at[slot],
            device_id=(my_bin, other) if axis == "sky" else (other, my_sky),
            device_id_type=MESH,
        )

    def each(n, mine, act):
        def body(k, carry):
            act(lax.rem(mine + k, n))
            return carry

        lax.fori_loop(1, n, body, 0)

    each(sky, my_sky, lambda o: along("sky", mark_ref, marks_ref, send_m, recv_m, o, my_sky).start())
    each(count, me, lambda o: window_copy(o, me).start())
    own_mark = pltpu.make_async_copy(mark_ref, marks_ref.at[my_sky], own_sem.at[0])
    own_mark.start()
    own = pltpu.make_async_copy(src_of(x_ref, me), y_ref.at[me], own_sem.at[1])
    own.start()

    tall = tap_ref.shape[3]
    row_hi, row_lo, back_hi, back_lo = [], [], [], []
    narrow = round_up(rows + 2 * half + 1, 128)
    for s in range(scales):
        taps, turned = tap_ref[0, s], tap_ref[1, s]
        for at, part in enumerate(halves(band(turned[:, :width], width, width, half, width))):
            col_ref[at, s] = part
        for at, part in enumerate(
            halves(band(taps[:, :span], span, span, half + halo, part_width))
        ):
            adj_ref[at, s] = part
        a, b = halves(band(taps[:, :narrow], rows, narrow, half, rows))
        row_hi.append(a)
        row_lo.append(b)
        back = band(turned[:, :narrow], rows, narrow, half, rows)
        back_hi.append(back)
    row_hi = jnp.concatenate(row_hi, axis=0)
    row_lo = jnp.concatenate(row_lo, axis=0)
    back = halves(jnp.concatenate(back_hi, axis=1))
    diag = same_row(size)
    lanes = lax.broadcasted_iota(jnp.int32, (size, width), 1)
    owned = (lanes >= halo) & (lanes < halo + chunk)
    spot = lax.rem(lax.broadcasted_iota(jnp.int32, (bins, size), 1), XB)
    bin_row = lax.broadcasted_iota(jnp.int32, (bins, size), 0)

    pairs = fit_ref.shape[1]
    first = jnp.broadcast_to(pair_ref[:, 0:1], (pairs, size))
    second = jnp.broadcast_to(pair_ref[:, 1:2], (pairs, size))
    right_hot = lax.broadcasted_iota(jnp.int32, (pairs, size), 1) // XB == second
    weight = jnp.zeros((bins, size), F32)
    target = jnp.zeros((bins, size), F32)
    for i in range(bins):
        hot = right_hot & (first == i)
        weight_row = jnp.sum(jnp.where(hot, fit_ref[0], 0.0), axis=0, keepdims=True)
        target_row = jnp.sum(jnp.where(hot, fit_ref[1], 0.0), axis=0, keepdims=True)
        weight = jnp.where(bin_row == i, weight_row, weight)
        target = jnp.where(bin_row == i, target_row, target)
    sums_ref[...] = jnp.zeros_like(sums_ref)

    each(sky, my_sky, lambda o: along("sky", mark_ref, marks_ref, send_m, recv_m, o, o).wait())
    own_mark.wait()
    each(count, me, lambda o: window_copy(o, o).wait())
    own.wait()

    mark_width = mark_ref.shape[1]
    start = me * chunk - halo + 128
    marks = marks_ref[...].reshape(rows, mark_width)
    marks = pltpu.roll(marks, lax.rem(mark_width - start // 128, mark_width), 1)
    which = (lax.broadcasted_iota(jnp.int32, (rows, width), 1) + start) // 128 - start // 128
    mask = jnp.zeros((rows, width), F32)
    for t in range(tiles):
        mask = jnp.where(which == t, jnp.broadcast_to(marks[:, t : t + 1], (rows, width)), mask)
    masks = [
        jnp.concatenate([mask[g * XB : (g + 1) * XB]] * bins, axis=0) > 0 for g in range(groups)
    ]

    for b in range(bins):
        y = jnp.concatenate([y_ref[b * sky + k].astype(F32) for k in range(sky)], axis=0)
        y = y.astype(BF16)
        hi, lo = halves(mm(row_hi, y) + mm(row_lo, y))
        for s in range(scales):
            for g in range(groups):
                part = slice(s * rows + g * XB, s * rows + (g + 1) * XB)
                hi_ref[g, s, b * XB : (b + 1) * XB, :] = hi[part]
                lo_ref[g, s, b * XB : (b + 1) * XB, :] = lo[part]

    for g in range(groups):

        def forward(s, carry):
            matrix = (col_ref[0, s], col_ref[1, s])
            filtered = mm3((hi_ref[g, s], lo_ref[g, s]), matrix).astype(BF16).astype(F32)
            kept = jnp.where(masks[g], filtered, 0.0)
            g_ref[g, s] = kept.astype(BF16)
            left = jnp.where(owned, kept, 0.0).astype(BF16)
            for l in range(lags):
                right = kept if l == 0 else pltpu.roll(kept, width - l, 1)
                gram = lax.dot_general(
                    left, right.astype(BF16), (((1,), (1,)), ((), ())), preferred_element_type=F32
                )
                gram = jnp.sum((gram * diag).reshape(bins, XB, size), axis=1)
                sums_ref[s * lags + l] = sums_ref[s * lags + l] + gram
            return carry

        lax.fori_loop(0, scales, forward, 0)

    table = jnp.zeros((bins, size), F32)
    for at in range(scales * lags):
        value = sums_ref[at]
        for step in (16, 8, 4, 2, 1):
            value = value + pltpu.roll(value, size - step, 1)
        if at:
            value = pltpu.roll(value, at, 1)
        table = jnp.where(spot == at, value, table)

    part_ref[...] = table
    each(sky, my_sky, lambda o: along("sky", part_ref, sky_ref, send_s, recv_s, o, my_sky).start())
    sky_ref[pl.ds(my_sky, 1)] = table[None]
    each(sky, my_sky, lambda o: along("sky", part_ref, sky_ref, send_s, recv_s, o, o).wait())
    table = sky_ref[0]
    for k in range(1, sky):
        table = table + sky_ref[k]
    bin_in_ref[...] = table
    each(bins, my_bin, lambda o: along("bin", bin_in_ref, bin_ref, send_b, recv_b, o, my_bin).start())
    bin_ref[pl.ds(my_bin, 1)] = table[None]
    each(bins, my_bin, lambda o: along("bin", bin_in_ref, bin_ref, send_b, recv_b, o, o).wait())
    table = bin_ref[0]
    for k in range(1, bins):
        table = table + bin_ref[k]
    table = table * area

    picked = jnp.zeros((pairs, size), F32)
    for i in range(bins):
        picked = jnp.where(first == i, jnp.broadcast_to(table[i : i + 1], (pairs, size)), picked)
    picked = jnp.where(right_hot, picked, 0.0)
    step = size // 2
    while step >= XB:
        picked = picked + pltpu.roll(picked, step, 1)
        step //= 2
    corr_ref[...] = picked

    ahead = jnp.where(spot < scales * lags, weight * (table - target), 0.0)
    spread = jnp.broadcast_to(ahead[:, None, :], (bins, XB, size)).reshape(size, size)
    behind = jnp.sum(jnp.transpose(spread * diag).reshape(bins, XB, size), axis=1)

    def coefficient(values, at):
        value = jnp.where(spot == at, values, 0.0)
        value = pltpu.roll(value, lax.rem(size - at, size), 1)
        for step in (1, 2, 4, 8, 16):
            value = value + pltpu.roll(value, step, 1)
        return value

    def grad_copy(piece, other, slot):
        return pltpu.make_async_remote_copy(
            src_ref=grad_ref.at[piece, other],
            dst_ref=dst_of(result_ref, slot, piece),
            send_sem=send_g.at[piece, other],
            recv_sem=recv_g.at[piece, slot],
            device_id=(other // sky, lax.rem(other, sky)),
            device_id_type=MESH,
        )

    own_grads = []
    for piece in range(pieces):
        cut = slice(piece * part_width, piece * part_width + span)
        for g in range(groups):

            def backward(s, carry):
                maps = g_ref[g, s, :, cut].astype(F32)
                total_grad = jnp.zeros((size, span), F32)
                for shift in range(1 - lags, lags):
                    moved = maps if shift == 0 else pltpu.roll(maps, (span - shift) % span, 1)
                    moved = moved.astype(BF16)
                    at = s * (2 * lags - 1) + shift + lags - 1
                    if piece == 0:
                        if shift == 0:
                            coef = coefficient(ahead + behind, s * lags)
                        elif shift > 0:
                            coef = coefficient(ahead, s * lags + shift)
                        else:
                            coef = coefficient(behind, s * lags - shift)
                        if pieces > 1 or groups > 1:
                            coef_ref[at] = coef
                    else:
                        coef = coef_ref[at]
                    full = jnp.broadcast_to(coef[:, None, :], (bins, XB, size))
                    hi, lo = halves(full.reshape(size, size) * diag)
                    total_grad = total_grad + mm(hi, moved) + mm(lo, moved)
                total_grad = jnp.where(masks[g][:, cut], total_grad, 0.0)
                hi, lo = halves(mm3(halves(total_grad), (adj_ref[0, s], adj_ref[1, s])))
                hi_ref[g, s, :, :part_width] = hi
                lo_ref[g, s, :, :part_width] = lo
                return carry

            lax.fori_loop(0, scales, backward, 0)

        for b in range(bins):
            spots = [(g, s) for s in range(scales) for g in range(groups)]
            rows_of = slice(b * XB, (b + 1) * XB)
            hi = jnp.concatenate([hi_ref[g, s, rows_of, :part_width] for g, s in spots], axis=0)
            lo = jnp.concatenate([lo_ref[g, s, rows_of, :part_width] for g, s in spots], axis=0)
            total_rows = mm3(back, (hi, lo))
            for k in range(sky):
                at = b * sky + k
                grad_ref[piece, at] = total_rows[k * strip_rows : (k + 1) * strip_rows]

        each(count, me, lambda o: grad_copy(piece, o, me).start())
        own_grad = pltpu.make_async_copy(
            grad_ref.at[piece, me], dst_of(result_ref, me, piece), own_sem.at[2 + piece]
        )
        own_grad.start()
        own_grads.append(own_grad)
    for piece in range(pieces):
        each(count, me, lambda o: grad_copy(piece, o, o).wait())
        own_grads[piece].wait()


def per_device(lensing_maps, filter_taps, survey_mask, bin_pairs, target_corr, pair_weight):
    scales, tap_count = filter_taps.shape
    half = (tap_count - 1) // 2
    strip = lensing_maps[0]
    strip_rows, cols = strip.shape
    bins, sky = lax.axis_size("bin"), lax.axis_size("sky")
    count = bins * sky
    pairs, lags = pair_weight.shape[0], pair_weight.shape[2]
    row_count = strip_rows * sky
    groups = row_count // XB
    chunk = cols // count
    width = round_up(chunk + 2 * (2 * half + lags - 1), 128)
    halo = (width - chunk) // 2
    out_width = round_up(chunk, 128)
    tiles = width // 128 + 1
    size = bins * XB
    aligned = chunk % 128 == 0
    pieces = out_width // 128
    part_width = out_width // pieces
    span = width - (pieces - 1) * part_width

    windows = jnp.pad(strip, ((0, 0), (halo, halo)))
    if not aligned:
        windows = jnp.stack([windows[:, d * chunk : d * chunk + width] for d in range(count)])
    mark_width = round_up(survey_mask.shape[1] + 1 + tiles, 128)
    marks = jnp.pad(
        survey_mask.astype(F32), ((0, 0), (1, mark_width - survey_mask.shape[1] - 1))
    )
    marks = jnp.broadcast_to(marks, (strip_rows, mark_width))
    tall = max(width, round_up(row_count + 2 * half + 1, 128))
    taps = jnp.stack([filter_taps, filter_taps[:, ::-1]])
    taps = jnp.pad(taps, ((0, 0), (0, 0), (0, tall - tap_count)))[:, :, None, :]
    fit = jnp.stack([pair_weight, target_corr]).reshape(2, pairs, scales * lags)
    fit = jnp.tile(jnp.pad(fit, ((0, 0), (0, 0), (0, XB - scales * lags))), (1, 1, bins))

    if aligned:
        src_of = lambda ref, d: ref.at[:, pl.ds(pl.multiple_of(d * chunk, 128), width)]
        dst_of = lambda ref, d, p: ref.at[
            :, pl.ds(pl.multiple_of(d * chunk + p * part_width, 128), part_width)
        ]
        result_shape = (strip_rows, cols)
    else:
        src_of = lambda ref, d: ref.at[d]
        dst_of = lambda ref, d, p: ref.at[d]
        result_shape = (count, strip_rows, out_width)

    spec = pl.BlockSpec(memory_space=pltpu.VMEM)
    table_shape = (bins, size)
    dma = pltpu.SemaphoreType.DMA
    result, corr = pl.pallas_call(
        functools.partial(
            step_kernel, bins, sky, scales, lags, groups, chunk, halo, tiles, half,
            1.0 / (row_count * cols), src_of, dst_of,
        ),
        out_shape=(
            jax.ShapeDtypeStruct(result_shape, F32),
            jax.ShapeDtypeStruct((pairs, size), F32),
        ),
        in_specs=[spec] * 5,
        out_specs=(spec, spec),
        scratch_shapes=[
            pltpu.VMEM((count, strip_rows, width), BF16),
            pltpu.VMEM((sky, strip_rows, mark_width), F32),
            pltpu.VMEM((groups, scales, size, width), BF16),
            pltpu.VMEM((groups, scales, size, width), BF16),
            pltpu.VMEM((groups, scales, size, width), BF16),
            pltpu.VMEM((scales * lags,) + table_shape, F32),
            pltpu.VMEM((pieces, count, strip_rows, part_width), F32),
            pltpu.VMEM((2, scales, width, width), BF16),
            pltpu.VMEM((2, scales, span, part_width), BF16),
            pltpu.VMEM(table_shape, F32),
            pltpu.VMEM((sky,) + table_shape, F32),
            pltpu.VMEM(table_shape, F32),
            pltpu.VMEM((bins,) + table_shape, F32),
            dma((count,)), dma((count,)), dma((sky,)), dma((sky,)), dma((sky,)), dma((sky,)),
            dma((bins,)), dma((bins,)), dma((pieces, count)), dma((pieces, count)), dma((2 + pieces,)),
            pltpu.VMEM((scales * (2 * lags - 1),) + table_shape, F32),
        ],
        compiler_params=pltpu.CompilerParams(
            collective_id=1, has_side_effects=True, vmem_limit_bytes=VMEM_LIMIT
        ),
    )(windows, marks, taps, bin_pairs, fit)
    if not aligned:
        result = jnp.transpose(result[:, :, :chunk], (1, 0, 2)).reshape(strip_rows, cols)
    corr_table = corr[:, : scales * lags].reshape(pairs, scales, lags)
    return (corr_table, result[None])


def solution(mesh):
    placed = (P("bin", "sky", None), P(), P("sky", None), P(), P(), P())
    return jax.shard_map(
        per_device,
        mesh=mesh,
        in_specs=placed,
        out_specs=(P(), P("bin", "sky", None)),
        check_vma=False,
    )
```
